32 devices in a mesh: groups: 2 (over y), sketch: 4 (over z), context: 2 (over x), example: 2 (over core).
Axes of the slice: x: 2, y: 2, z: 4, core: 2. Of those that a mesh axis runs over, the one named last changes fastest.
Arguments:
- activations: bfloat16 [8, 4096, 512], P('groups', ('sketch', 'context')), parts along dimension 0, may hold values from -6 to 6
- out_grads: bfloat16 [8, 4096, 512], P('groups', ('sketch', 'example')), parts along dimension 0, may hold values from -6 to 6
- sign_bits: int32 [4, 2, 512, 2, 128], P(None, 'context', None, 'example'), may hold values from 0 to 65535
- keep_cols: int32 [128], replicated, may hold values from 0 to 31
- row_start: int32 [128], P(('context', 'example')), may hold values from 0 to 4095
- row_step: int32 [128], P(('context', 'example')), may hold values from 0 to 2047
- val_sketch: float32 [64, 8192], P('sketch', ('context', 'example')), may hold values from -6 to 6
Outputs:
- scores: float32 [8, 64], P(('groups', 'sketch')), parts along dimension 0
The draws below stay inside these ranges and needn't reach their ends.
There are 2 independent parts, one for each index of `groups`. The reference program is written for one: setup_inputs(seed, part) draws one part's arguments, and reference() takes and returns one part's arrays. A program takes and returns all parts, laid end to end along the dimension named above; an argument that names none is the same for every part. Nothing has to cross between parts.
Inputs may be any that keep to these rules, and one draw needn't show every extreme that they name: `sign_bits`: each word holds 16 independent fair sign bits in its low 16 bits.
All inputs are finite; a program needn't handle non-finite values.
Results may differ from the reference program's by a relative error of at most 0.0003.
Values may be sent and summed in bfloat16 or wider, within the bound.
No kernel may reach another device: no remote copies, remote signals or barrier semaphores. Data moves between devices by JAX's collectives and lax.ppermute only.
A program may use at most 128 MiB of HBM per device.

```python
import math
import jax
import jax.numpy as jnp
from jax import lax

DI = 4096
DO = 4096
TOKENS = 512
KR = 64
KC = 128
NV = 64
EXAMPLES = 4
RK = 512
WK = 512
KEEP = 8192
N_SKETCH = 4
N_CONTEXT = 2
N_EXAMPLE = 2


def place_ends(values, rng, smallest, top_value):
    shape = values.shape
    spot = [jax.random.randint(jax.random.fold_in(rng, axis), (), 0, shape[axis]) for axis in range(len(shape))]
    values = values.at[tuple(spot)].set(smallest)
    longest = shape.index(max(shape))
    spot[longest] = (spot[longest] + 1) % shape[longest]
    return values.at[tuple(spot)].set(top_value)


def level_of(stream_key, extent, shards, low, top_value):
    level = 1.0
    for axis_at, parts in shards:
        heights = jax.random.uniform(jax.random.fold_in(jax.random.fold_in(stream_key, 6), axis_at), (parts,), jnp.float32, low / len(shards), top_value / len(shards))
        level = level * jnp.repeat(jnp.exp(heights), extent[axis_at] // parts).reshape((-1,) + (1,) * (len(extent) - 1 - axis_at))
    return level


def bell_draw(rng, shape, spread, most, pieces=(), kind=jnp.bfloat16):
    result = jax.random.normal(rng, shape, jnp.float32) * spread
    if len(pieces) > 0:
        result = level_of(rng, shape, pieces, -0.22, 0.18) * result
    return jnp.clip(result, min=-most, max=most).astype(kind)


def setup_inputs(seed: int = 0, part: int = 0) -> dict:
    streams_of = jax.random.split(jax.random.key(seed), 8)
    part_splits = jax.random.split(jax.random.fold_in(streams_of[7], part), 8)
    return {
        "activations": bell_draw(part_splits[0], (EXAMPLES, DI, TOKENS), 1.0, 6.0, ((1, 8),)),
        "out_grads": bell_draw(part_splits[1], (EXAMPLES, DO, TOKENS), 1.0, 6.0, ((1, 8),)),
        "sign_bits": place_ends(jax.random.randint(streams_of[2], (N_SKETCH, N_CONTEXT, RK, N_EXAMPLE, N_SKETCH * WK // 16), 0, 65536), jax.random.fold_in(streams_of[2], 1), 0, 65535).astype(jnp.int32),
        "keep_cols": place_ends(jax.random.randint(streams_of[3], (KC,), 0, DO // KC), jax.random.fold_in(streams_of[3], 1), 0, (DO // KC) - 1).astype(jnp.int32),
        "row_start": place_ends(jax.random.randint(streams_of[4], (KC,), 0, DI), jax.random.fold_in(streams_of[4], 1), 0, DI - 1).astype(jnp.int32),
        "row_step": place_ends(jax.random.randint(streams_of[5], (KC,), 0, DI // 2), jax.random.fold_in(streams_of[5], 1), 0, (DI // 2) - 1).astype(jnp.int32),
        "val_sketch": bell_draw(streams_of[6], (NV, KEEP), 1.0, 6.0, ((0, 4), (1, 4)), jnp.float32),
    }


def parity_sign(common, length):
    ones_total = jnp.zeros(common.shape, jnp.int32)
    for bit_place in range(max(length.bit_length() - 1, 1)):
        ones_total = ones_total + jnp.bitwise_and(jnp.right_shift(common, bit_place), 1)
    return (1 - 2 * jnp.bitwise_and(ones_total, 1)).astype(jnp.float32)

def hadamard_table(length):
    positions = jnp.arange(length, dtype=jnp.int32)
    common = jnp.bitwise_and(positions[:, None], positions[None, :])
    return parity_sign(common, length)

def hadamard_last(values):
    length = values.shape[-1]
    inner_len = min(128, length)
    outer_len = length // inner_len
    leading = values.shape[:-1]
    blocks = values.reshape(leading + (outer_len, inner_len))
    blocks = jnp.einsum('...ab,bc->...ac', blocks, hadamard_table(inner_len), precision=lax.Precision.HIGHEST)
    blocks = jnp.einsum('...ab,ac->...cb', blocks, hadamard_table(outer_len), precision=lax.Precision.HIGHEST)
    return blocks.reshape(values.shape) * (1.0 / math.sqrt(length))

def sign_table(packed):
    places = jnp.arange(16, dtype=jnp.int32)
    bit_values = jnp.bitwise_and(jnp.right_shift(packed[..., None], places), 1)
    return (1 - 2 * bit_values).astype(jnp.float32).reshape(packed.shape[:-1] + (packed.shape[-1] * 16,))

def reference(activations, out_grads, sign_bits, keep_cols, row_start, row_step, val_sketch):
    words = sign_bits.reshape(DI, N_EXAMPLE, N_SKETCH, WK // 16)
    words = jnp.transpose(words, (0, 2, 1, 3)).reshape(DI, DO // 16)
    sign_grid = sign_table(words)
    kept_count = keep_cols.shape[0]
    width_block = DO // kept_count
    columns = (jnp.arange(kept_count, dtype=jnp.int32) * width_block + keep_cols).astype(jnp.int32)
    strides = 2 * row_step + 1
    kept_rows = ((row_start[:, None] + jnp.arange(KR, dtype=jnp.int32)[None, :] * strides[:, None]) % DI).astype(jnp.int32)

    def one_example(example_pair):
        act_rows, grad_rows = example_pair
        gradient = lax.dot_general(act_rows, grad_rows, (((1,), (1,)), ((), ())), preferred_element_type=jnp.float32)
        transformed = hadamard_last(sign_grid * gradient)
        picked = jnp.take(transformed, columns, axis=1).T
        picked = hadamard_last(picked)
        return jnp.take_along_axis(picked, kept_rows, axis=1).reshape(-1)
    sketch = lax.map(one_example, (activations, out_grads))
    products = jnp.dot(sketch, val_sketch.T, precision=lax.Precision.HIGHEST)
    norm_sq = lax.optimization_barrier(jnp.sum(sketch * sketch, axis=1))
    return products / jnp.sqrt(norm_sq + 1e-06)[:, None]
```

```python
import functools
import math

import jax
import jax.numpy as jnp
from jax import lax
from jax.experimental import pallas as pl
from jax.experimental.pallas import tpu as pltpu
from jax.sharding import PartitionSpec as P

KR = 64
LANES = 128
BITS = 16
VMEM = pl.BlockSpec(memory_space=pltpu.VMEM)
SMEM = pl.BlockSpec(memory_space=pltpu.SMEM)
NT = (((1,), (1,)), ((), ()))
GRANT = pltpu.CompilerParams(vmem_limit_bytes=20 * 2**20)


def parity_sign(common, length):
    ones_total = jnp.zeros(common.shape, jnp.int32)
    for bit_place in range(max(length.bit_length() - 1, 1)):
        ones_total = ones_total + jnp.bitwise_and(jnp.right_shift(common, bit_place), 1)
    return (1 - 2 * jnp.bitwise_and(ones_total, 1)).astype(jnp.float32)


def hadamard_table(length):
    positions = jnp.arange(length, dtype=jnp.int32)
    common = jnp.bitwise_and(positions[:, None], positions[None, :])
    return parity_sign(common, length)


def hadamard_last(values):
    length = values.shape[-1]
    inner_len = min(128, length)
    outer_len = length // inner_len
    leading = values.shape[:-1]
    blocks = values.reshape(leading + (outer_len, inner_len))
    blocks = jnp.einsum(
        "...ab,bc->...ac", blocks, hadamard_table(inner_len), precision=lax.Precision.HIGHEST
    )
    blocks = jnp.einsum(
        "...ab,ac->...cb", blocks, hadamard_table(outer_len), precision=lax.Precision.HIGHEST
    )
    return blocks.reshape(values.shape) * (1.0 / math.sqrt(length))


def sign_table(packed):
    places = jnp.arange(16, dtype=jnp.int32)
    bit_values = jnp.bitwise_and(jnp.right_shift(packed[..., None], places), 1)
    return (
        (1 - 2 * bit_values)
        .astype(jnp.float32)
        .reshape(packed.shape[:-1] + (packed.shape[-1] * 16,))
    )


def plain_body(activations, out_grads, sign_bits, keep_cols, row_start, row_step, val_sketch):
    sketch_count = lax.axis_size("sketch")
    context_count = lax.axis_size("context")
    example_count = lax.axis_size("example")
    example_index = lax.axis_index("example")
    feature_piece = activations.shape[1]
    column_piece = out_grads.shape[1]
    in_width = feature_piece * sketch_count * context_count
    out_width = column_piece * sketch_count * example_count
    local_width = column_piece * sketch_count
    kept_count = keep_cols.shape[0]
    block_width = out_width // kept_count
    columns = jnp.arange(kept_count, dtype=jnp.int32) * block_width + keep_cols
    arrived_in, arrived_out = (
        lax.all_to_all(activations, "sketch", split_axis=0, concat_axis=1, tiled=True),
        lax.all_to_all(out_grads, "sketch", split_axis=0, concat_axis=1, tiled=True),
    )
    gradient = jnp.einsum(
        "edt,ekt->dk", arrived_in, arrived_out, preferred_element_type=jnp.float32
    )
    words = sign_bits.reshape(sketch_count * feature_piece, -1)
    signed = gradient * sign_table(words)
    positions = jnp.arange(local_width, dtype=jnp.int32)
    global_cols = (
        positions // column_piece * example_count + example_index
    ) * column_piece + positions % column_piece
    common = jnp.bitwise_and(global_cols[:, None], columns[None, :])
    col_table = parity_sign(common, out_width) * (1.0 / math.sqrt(out_width))
    partial_value = jnp.dot(signed, col_table, precision=lax.Precision.HIGHEST)
    rows_local = signed.shape[0]
    per_device = kept_count // (context_count * example_count)
    split_cols = partial_value.reshape(rows_local, context_count, example_count, per_device)
    moved_parts = lax.all_to_all(split_cols, "context", split_axis=1, concat_axis=0, tiled=True)
    whole_rows = lax.psum_scatter(moved_parts, "example", scatter_dimension=2, tiled=True)
    ordered = whole_rows.reshape(context_count, sketch_count, feature_piece, per_device)
    ordered = jnp.transpose(ordered, (1, 0, 2, 3)).reshape(in_width, per_device)
    column = hadamard_last(ordered.T)
    strides = 2 * row_step + 1
    kept_rows = (
        row_start[:, None] + jnp.arange(KR, dtype=jnp.int32)[None, :] * strides[:, None]
    ) % in_width
    own_sketch = jnp.take_along_axis(column, kept_rows, axis=1).reshape(1, -1)
    products = jnp.dot(
        own_sketch,
        lax.all_gather(val_sketch, "sketch", axis=0, tiled=True).T,
        precision=lax.Precision.HIGHEST,
    )
    squares = jnp.sum(own_sketch * own_sketch, axis=1)
    products, squares = lax.psum((products, squares), ("context", "example"))
    return products / jnp.sqrt(squares + 1e-06)[:, None]


def odd(values):
    for shift in (8, 4, 2, 1):
        values = jnp.bitwise_xor(values, jnp.right_shift(values, shift))
    return jnp.bitwise_and(values, 1) == 1


def split(values):
    high = values.astype(jnp.bfloat16)
    return high, (values - high.astype(jnp.float32)).astype(jnp.bfloat16)


def dot(left, right):
    return jnp.dot(left, right, preferred_element_type=jnp.float32)


def table_kernel(spots, words, keep, turned, table, low):
    pieces, rows, _ = words.shape
    tiles, kept, width = table.shape
    halves = tiles // pieces
    block = spots[2]
    for piece in range(pieces):
        turned[piece] = words[piece].T
    columns = lax.broadcasted_iota(jnp.int32, (kept, 1), 0)
    half_kept = kept // 2
    columns = jnp.where(columns < half_kept, 2 * columns, 2 * (columns - half_kept) + 1) * block + keep[...]
    offsets = lax.broadcasted_iota(jnp.int32, (1, width), 1)
    for tile in range(tiles):
        piece, half = tile // halves, tile % halves
        first = ((piece * spots[1] + spots[0]) * halves + half) * width
        common = jnp.bitwise_and(first + offsets, columns)
        table[tile] = jnp.where(odd(common), -1.0, 1.0).astype(jnp.bfloat16)
    place_row = lax.broadcasted_iota(jnp.int32, (LANES, LANES), 0)
    place_col = lax.broadcasted_iota(jnp.int32, (LANES, LANES), 1)
    entry = jnp.where(odd(jnp.bitwise_and(jnp.bitwise_and(place_row, place_col), KR - 1)), -1.0, 1.0)
    low[...] = jnp.where(place_row // KR == place_col // KR, entry, 0.0).astype(jnp.bfloat16)


def kept_kernel(length, starts, steps, signs, order):
    kept = starts.shape[0]
    lane = lax.broadcasted_iota(jnp.int32, (kept, LANES), 1)
    low = jnp.bitwise_and(lane, KR - 1)
    stride = 2 * steps[...] + 1
    inverse = stride * (2 - stride * stride)
    index = jnp.bitwise_and((low - starts[...]) * inverse, KR - 1)
    high = jnp.right_shift(jnp.bitwise_and(starts[...] + index * stride, length - 1), KR.bit_length() - 1)
    for bit in range(signs.shape[0]):
        signs[bit] = jnp.where(jnp.bitwise_and(jnp.right_shift(high, bit), 1) == 1, -1.0, 1.0)
    half = kept // 2
    where = jnp.bitwise_and(starts[...] + low * stride, KR - 1) + lane - low
    order[...] = jnp.where(lane[:half] < KR, where[:half], where[half:])


def piece_kernel(row_sizes, col_sizes, first, last, total_scale, *refs):
    spots, refs = refs[0], refs[1:]
    rows, refs = refs[: len(row_sizes)], refs[len(row_sizes) :]
    cols, refs = refs[: len(col_sizes)], refs[len(col_sizes) :]
    turned, table, low, signs, refs = refs[0], refs[1], refs[2], refs[3], refs[4:]
    if not first:
        before, refs = refs[0], refs[1:]
    if last:
        order, refs = refs[0], refs[1:]
    out, gathered, projected = refs
    height = gathered.shape[0]
    width = table.shape[2]
    row_piece = spots[0]
    for number, size in enumerate(row_sizes):
        if size == height:
            gathered[...] = rows[number][...].reshape(gathered.shape)
        else:
            gathered[pl.ds(pl.multiple_of(spots[2 + number] * size, size), size), :] = rows[number][...]
    bit = jnp.left_shift(1, lax.broadcasted_iota(jnp.int32, (1, BITS, 1), 1))
    word_rows = width // BITS
    place = 2 + len(row_sizes)
    done = 0
    for number, size in enumerate(col_sizes):
        for inner in range(size // width):
            tile = spots[place + number] + inner
            if len(cols[number].shape) == 3:
                block = cols[number][0, inner * width : (inner + 1) * width, :]
            else:
                block = cols[number][inner * width : (inner + 1) * width, :]
            gradient = lax.dot_general(block, gathered[...], NT, preferred_element_type=jnp.float32)
            words = turned[row_piece, pl.ds(pl.multiple_of(tile * word_rows, word_rows), word_rows), :]
            flips = jnp.bitwise_and(words[:, None, :], bit).reshape(width, height) != 0
            high, rest = split(jnp.where(flips, -gradient, gradient))
            entries = table[tile]
            part = dot(entries, high) + dot(entries, rest)
            if done == 0:
                projected[...] = part
            else:
                projected[...] += part
            done += 1
    groups = []
    for group in range(height // LANES):
        high, rest = split(projected[:, group * LANES : (group + 1) * LANES])
        groups.append(dot(high, low[...]) + dot(rest, low[...]))
    level = 1
    while len(groups) > 1:
        groups = [groups[at] + signs[level] * groups[at + 1] for at in range(0, len(groups), 2)]
        level += 1
    value = groups[0]
    lane = lax.broadcasted_iota(jnp.int32, value.shape, 1)
    value = jnp.where(lane >= KR, signs[0] * value, value)
    spot = row_piece * spots[1] + spots[len(row_sizes) + 2 + len(col_sizes)]
    for bit_at in range(level, signs.shape[0]):
        turn = jnp.bitwise_and(jnp.right_shift(spot, bit_at - level), 1).astype(jnp.float32)
        value = value + turn * (signs[bit_at] * value - value)
    if not first:
        value = before[...] + value
    if last:
        value = (value + pltpu.roll(value, KR, 1)) * total_scale
        half = value.shape[0] // 2
        value = jnp.where(lane[:half] < KR, value[:half], value[half:])
        value = jnp.take_along_axis(value, order[...], axis=1)
        value = value.reshape(out.shape)
    out[...] = value


def add_piece(spots, rows, row_sizes, cols, col_sizes, turned, table, low, signs, before, order, scale, owners):
    height, tokens = sum(row_sizes), rows[0].shape[-1]
    kept = table.shape[1]
    first, last = before is None, order is not None
    operands = [spots, *rows, *cols, turned, table, low, signs]
    operands += [] if first else [before]
    operands += [order] if last else []
    specs = [SMEM]
    for array in operands[1:]:
        specs.append(VMEM)
    shape = (owners, kept // 2 // owners, LANES) if last else (kept, LANES)
    width = sum(col_sizes)
    return pl.pallas_call(
        functools.partial(piece_kernel, tuple(row_sizes), tuple(col_sizes), first, last, scale),
        out_shape=jax.ShapeDtypeStruct(shape, jnp.float32),
        in_specs=specs,
        out_specs=VMEM,
        scratch_shapes=[pltpu.VMEM((height, tokens), jnp.bfloat16), pltpu.VMEM((kept, height), jnp.float32)],
        compiler_params=GRANT,
        cost_estimate=pl.CostEstimate(
            flops=2 * height * width * (tokens + 2 * kept), bytes_accessed=2 * tokens * (height + width), transcendentals=0
        ),
    )(*operands)


def product_body(parts_count, vals_count, spots, *refs):
    parts, vals, out, wide = refs[:parts_count], refs[parts_count : parts_count + vals_count], refs[-2], refs[-1]
    terms = [parts[0][spots[1]]] + [part[...] for part in parts[1:]]
    while len(terms) > 1:
        terms = [terms[at] + terms[at + 1] for at in range(0, len(terms), 2)]
    own = terms[0]
    wide[...] = jnp.zeros_like(wide)
    each = vals[0].shape[0]
    for number in range(vals_count):
        total = jnp.zeros((each, LANES), jnp.float32)
        for group in range(own.shape[0]):
            total += own[group : group + 1] * vals[number][:, group * LANES : (group + 1) * LANES]
        first = pl.multiple_of(jnp.bitwise_xor(spots[0], number) * each, each)
        wide[pl.ds(first, each), :] = total
    wide[each * vals_count : each * vals_count + 1, :] = jnp.sum(own * own, axis=0, keepdims=True)
    out[...] = jnp.sum(wide[...].T, axis=0, keepdims=True)


def swap(array, axes, size, key):
    return lax.ppermute(array, axes, [(at, at ^ key) for at in range(size)])


def fast_body(activations, out_grads, sign_bits, keep_cols, row_start, row_step, val_sketch):
    sketch_count = lax.axis_size("sketch")
    context_count = lax.axis_size("context")
    example_count = lax.axis_size("example")
    sketch_index = lax.axis_index("sketch")
    context_index = lax.axis_index("context")
    example_index = lax.axis_index("example")
    row_piece, tokens = activations.shape[1:]
    col_piece = out_grads.shape[1]
    in_width = row_piece * sketch_count * context_count
    out_width = col_piece * sketch_count * example_count
    kept = keep_cols.shape[0]
    owners = context_count * example_count
    owner = context_index * example_count + example_index
    row_half, col_half = row_piece // example_count, col_piece // context_count
    keys = list(range(1, sketch_count))
    ahead = keys[1:] + keys[:1]

    def share(array, key, index, size):
        start = (jnp.bitwise_xor(sketch_index, key), index * size, 0)
        return lax.dynamic_slice(array, start, (1, size, tokens)).reshape(size, tokens)

    got_out, got_in = {}, {}
    for key in ahead:
        got_out[key] = swap(share(out_grads, key, context_index, col_half), "sketch", sketch_count, key)
    for key in ahead:
        got_in[key] = swap(share(activations, key, example_index, row_half), "sketch", sketch_count, key)

    whole = ("context", "example")
    params = jnp.stack([row_start, row_step])
    val_sketch, params = lax.optimization_barrier((val_sketch, params, got_out[ahead[0]]))[:2]
    param_parts = jnp.stack([params] + [swap(params, whole, owners, key) for key in range(1, owners)])
    vals = [val_sketch] + [swap(val_sketch, "sketch", sketch_count, key) for key in keys]

    spots = jnp.stack([example_index, jnp.int32(example_count), jnp.int32(out_width // kept)]).astype(jnp.int32)
    words = sign_bits.reshape(sketch_count, row_piece, -1)
    places = jnp.bitwise_xor(owner, jnp.arange(owners, dtype=jnp.int32))
    chosen = (places[:, None] == jnp.arange(owners, dtype=jnp.int32)[None, :])[:, :, None, None]
    params = jnp.sum(jnp.where(chosen, param_parts[None], 0), axis=1)
    params = jnp.transpose(params, (1, 0, 2)).reshape(2, kept // 2, 2)
    params = jnp.transpose(params, (0, 2, 1)).reshape(2, kept, 1)
    keep = jnp.transpose(keep_cols.reshape(kept // 2, 2)).reshape(kept, 1)

    tiles = sketch_count * context_count
    turned, table, low = pl.pallas_call(
        table_kernel,
        out_shape=(
            jax.ShapeDtypeStruct((sketch_count, words.shape[2], row_piece), jnp.int32),
            jax.ShapeDtypeStruct((tiles, kept, col_half), jnp.bfloat16),
            jax.ShapeDtypeStruct((LANES, LANES), jnp.bfloat16),
        ),
        in_specs=[SMEM, VMEM, VMEM],
        out_specs=(VMEM, VMEM, VMEM),
        compiler_params=GRANT,
    )(spots, words, keep)
    high_bits = (in_width // KR).bit_length() - 1
    signs, order = pl.pallas_call(
        functools.partial(kept_kernel, in_width),
        out_shape=(
            jax.ShapeDtypeStruct((high_bits, kept, LANES), jnp.float32),
            jax.ShapeDtypeStruct((kept // 2, LANES), jnp.int32),
        ),
        in_specs=[VMEM, VMEM],
        out_specs=(VMEM, VMEM),
        compiler_params=GRANT,
    )(params[0], params[1])

    col_tiles, col_spots = {}, {}
    for key in ahead:
        piece = jnp.bitwise_xor(sketch_index, key)
        for shift in range(context_count):
            tile = got_out[key] if shift == 0 else swap(got_out[key], "context", context_count, shift)
            col_tiles[key, shift] = tile
            col_spots[key, shift] = piece * context_count + jnp.bitwise_xor(context_index, shift)
    own_in = lax.dynamic_slice(activations, (sketch_index, 0, 0), (1, row_piece, tokens))[0]
    own_out = lax.dynamic_slice(out_grads, (sketch_index, 0, 0), (1, col_piece, tokens))[0]

    def piece_of(key, rows, row_sizes, cols, before, order=None):
        place = jnp.stack(
            [jnp.bitwise_xor(sketch_index, key), jnp.int32(context_count)]
            + [jnp.bitwise_xor(example_index, shift) for shift in range(len(rows))]
            + [spot for _, spot in cols]
            + [context_index]
        ).astype(jnp.int32)
        return add_piece(
            place, rows, row_sizes, [tile for tile, _ in cols], [tile.shape[-2] for tile, _ in cols],
            turned, table, low, signs, before, order, 1.0 / math.sqrt(in_width * out_width), owners,
        )

    own_cols = [(own_out, sketch_index * context_count)]
    far_cols = [(col_tiles[at], col_spots[at]) for at in col_tiles]
    total = piece_of(0, [own_in], [row_piece], own_cols, None)
    total = piece_of(0, [own_in], [row_piece], far_cols, total)
    turns = keys[:1] + keys[1:]
    for key in turns:
        rows = [got_in[key]] + [swap(got_in[key], "example", example_count, shift) for shift in range(1, example_count)]
        total = piece_of(
            key, rows, [row_half] * example_count, own_cols + far_cols, total, order if key == turns[-1] else None
        )

    parts = [total]
    for key in range(1, owners):
        to = lax.dynamic_index_in_dim(total, jnp.bitwise_xor(owner, key), keepdims=False)
        parts.append(swap(to, whole, owners, key))
    sums = pl.pallas_call(
        functools.partial(product_body, owners, sketch_count),
        out_shape=jax.ShapeDtypeStruct((1, LANES), jnp.float32),
        in_specs=[SMEM] + [VMEM] * (owners + sketch_count),
        out_specs=VMEM,
        scratch_shapes=[pltpu.VMEM((LANES, LANES), jnp.float32)],
        compiler_params=GRANT,
    )(jnp.stack([sketch_index, owner]).astype(jnp.int32), *parts, *vals)
    terms = [sums] + [swap(sums, whole, owners, key) for key in range(1, owners)]
    while len(terms) > 1:
        terms = [terms[at] + terms[at + 1] for at in range(0, len(terms), 2)]
    count = val_sketch.shape[0] * sketch_count
    return terms[0][:, :count] / jnp.sqrt(terms[0][:, count : count + 1] + 1e-06)


def fits(mesh, activations, out_grads, keep_cols, val_sketch):
    sizes = mesh.shape
    rows = activations.shape[1] // (sizes["sketch"] * sizes["context"])
    cols = out_grads.shape[1] // (sizes["sketch"] * sizes["example"])
    owners = sizes["context"] * sizes["example"]
    powers = all(size & (size - 1) == 0 for size in (*sizes.values(), rows, cols, keep_cols.shape[0]))
    whole = rows % LANES == 0 and rows // sizes["example"] >= LANES and cols // sizes["context"] >= LANES
    one = activations.shape[0] == sizes["groups"] * sizes["sketch"]
    return (
        powers and whole and one and keep_cols.shape[0] == LANES and LANES // 2 // owners >= 8
        and val_sketch.shape[0] < LANES and val_sketch.shape[0] // sizes["sketch"] >= 8
    )


def solution(mesh):
    placed = (
        P("groups", ("sketch", "context"), None),
        P("groups", ("sketch", "example"), None),
        P(None, "context", None, "example", None),
        P(),
        P(("context", "example")),
        P(("context", "example")),
        P("sketch", ("context", "example")),
    )

    def whole(*arrays):
        body = fast_body if fits(mesh, arrays[0], arrays[1], arrays[3], arrays[6]) else plain_body
        return jax.shard_map(
            body, mesh=mesh, in_specs=placed, out_specs=P(("groups", "sketch"), None), check_vma=False
        )(*arrays)

    return whole
```

```python
import functools
import math

import jax
import jax.numpy as jnp
from jax import lax
from jax.experimental import pallas as pl
from jax.experimental.pallas import tpu as pltpu
from jax.sharding import PartitionSpec as P

KR = 64
LANES = 128
BITS = 16
VMEM = pl.BlockSpec(memory_space=pltpu.VMEM)
HBM = pl.BlockSpec(memory_space=pltpu.HBM)
NT = (((1,), (1,)), ((), ()))
GRANT = pltpu.CompilerParams(vmem_limit_bytes=20 * 2**20)


def parity_sign(common, length):
    ones_total = jnp.zeros(common.shape, jnp.int32)
    for bit_place in range(max(length.bit_length() - 1, 1)):
        ones_total = ones_total + jnp.bitwise_and(jnp.right_shift(common, bit_place), 1)
    return (1 - 2 * jnp.bitwise_and(ones_total, 1)).astype(jnp.float32)


def hadamard_table(length):
    positions = jnp.arange(length, dtype=jnp.int32)
    common = jnp.bitwise_and(positions[:, None], positions[None, :])
    return parity_sign(common, length)


def hadamard_last(values):
    length = values.shape[-1]
    inner_len = min(128, length)
    outer_len = length // inner_len
    leading = values.shape[:-1]
    blocks = values.reshape(leading + (outer_len, inner_len))
    blocks = jnp.einsum(
        "...ab,bc->...ac", blocks, hadamard_table(inner_len), precision=lax.Precision.HIGHEST
    )
    blocks = jnp.einsum(
        "...ab,ac->...cb", blocks, hadamard_table(outer_len), precision=lax.Precision.HIGHEST
    )
    return blocks.reshape(values.shape) * (1.0 / math.sqrt(length))


def sign_table(packed):
    places = jnp.arange(16, dtype=jnp.int32)
    bit_values = jnp.bitwise_and(jnp.right_shift(packed[..., None], places), 1)
    return (
        (1 - 2 * bit_values)
        .astype(jnp.float32)
        .reshape(packed.shape[:-1] + (packed.shape[-1] * 16,))
    )


def plain_body(activations, out_grads, sign_bits, keep_cols, row_start, row_step, val_sketch):
    sketch_count = lax.axis_size("sketch")
    context_count = lax.axis_size("context")
    example_count = lax.axis_size("example")
    example_index = lax.axis_index("example")
    feature_piece = activations.shape[1]
    column_piece = out_grads.shape[1]
    in_width = feature_piece * sketch_count * context_count
    out_width = column_piece * sketch_count * example_count
    local_width = column_piece * sketch_count
    kept_count = keep_cols.shape[0]
    block_width = out_width // kept_count
    columns = jnp.arange(kept_count, dtype=jnp.int32) * block_width + keep_cols
    arrived_in, arrived_out = (
        lax.all_to_all(activations, "sketch", split_axis=0, concat_axis=1, tiled=True),
        lax.all_to_all(out_grads, "sketch", split_axis=0, concat_axis=1, tiled=True),
    )
    gradient = jnp.einsum(
        "edt,ekt->dk", arrived_in, arrived_out, preferred_element_type=jnp.float32
    )
    words = sign_bits.reshape(sketch_count * feature_piece, -1)
    signed = gradient * sign_table(words)
    positions = jnp.arange(local_width, dtype=jnp.int32)
    global_cols = (
        positions // column_piece * example_count + example_index
    ) * column_piece + positions % column_piece
    common = jnp.bitwise_and(global_cols[:, None], columns[None, :])
    col_table = parity_sign(common, out_width) * (1.0 / math.sqrt(out_width))
    partial_value = jnp.dot(signed, col_table, precision=lax.Precision.HIGHEST)
    rows_local = signed.shape[0]
    per_device = kept_count // (context_count * example_count)
    split_cols = partial_value.reshape(rows_local, context_count, example_count, per_device)
    moved_parts = lax.all_to_all(split_cols, "context", split_axis=1, concat_axis=0, tiled=True)
    whole_rows = lax.psum_scatter(moved_parts, "example", scatter_dimension=2, tiled=True)
    ordered = whole_rows.reshape(context_count, sketch_count, feature_piece, per_device)
    ordered = jnp.transpose(ordered, (1, 0, 2, 3)).reshape(in_width, per_device)
    column = hadamard_last(ordered.T)
    strides = 2 * row_step + 1
    kept_rows = (
        row_start[:, None] + jnp.arange(KR, dtype=jnp.int32)[None, :] * strides[:, None]
    ) % in_width
    own_sketch = jnp.take_along_axis(column, kept_rows, axis=1).reshape(1, -1)
    products = jnp.dot(
        own_sketch,
        lax.all_gather(val_sketch, "sketch", axis=0, tiled=True).T,
        precision=lax.Precision.HIGHEST,
    )
    squares = jnp.sum(own_sketch * own_sketch, axis=1)
    products, squares = lax.psum((products, squares), ("context", "example"))
    return products / jnp.sqrt(squares + 1e-06)[:, None]


def odd(values):
    for shift in (8, 4, 2, 1):
        values = jnp.bitwise_xor(values, jnp.right_shift(values, shift))
    return jnp.bitwise_and(values, 1) == 1


def split(values):
    high = values.astype(jnp.bfloat16)
    return high, (values - high.astype(jnp.float32)).astype(jnp.bfloat16)


def dot(left, right):
    return jnp.dot(left, right, preferred_element_type=jnp.float32)


def upright(row, height):
    wide = (height, row.shape[1])
    lane, sublane = lax.broadcasted_iota(jnp.int32, wide, 1), lax.broadcasted_iota(jnp.int32, wide, 0)
    chosen = jnp.where(lane == sublane, row.astype(jnp.float32), 0.0)
    return jnp.sum(chosen, axis=1, keepdims=True).astype(jnp.int32)


def place():
    return lax.axis_index("sketch"), lax.axis_index("context"), lax.axis_index("example")


def share_kernel(keys, axis, array, *refs):
    outs, sems = refs[: len(keys)], refs[len(keys)]
    sketch_index, index = lax.axis_index("sketch"), lax.axis_index(axis)
    copies = []
    for number, key in enumerate(keys):
        size = outs[number].shape[0]
        rows = pl.ds(pl.multiple_of(index * size, size), size)
        source = array.at[jnp.bitwise_xor(sketch_index, key), rows, :]
        copies.append(pltpu.make_async_copy(source, outs[number], sems.at[number]))
    for copy in copies:
        copy.start()
    for copy in copies:
        copy.wait()


def share(array, keys, axis, size):
    return pl.pallas_call(
        functools.partial(share_kernel, keys, axis),
        out_shape=[jax.ShapeDtypeStruct((size, array.shape[2]), array.dtype)] * len(keys),
        in_specs=[HBM],
        out_specs=[VMEM] * len(keys),
        scratch_shapes=[pltpu.SemaphoreType.DMA((len(keys),))],
        compiler_params=GRANT,
        name="share",
    )(array)


def table_kernel(example_count, block, words, keep, activations, out_grads, *refs):
    turned, table, low, own_in, own_out, loaded, sems = refs
    pieces = words.shape[0]
    tiles, kept, width = table.shape
    halves = tiles // pieces
    sketch_index, _, example_index = place()
    first = pltpu.make_async_copy(words, loaded, sems.at[0])
    second = pltpu.make_async_copy(activations.at[sketch_index], own_in, sems.at[1])
    third = pltpu.make_async_copy(out_grads.at[sketch_index], own_out, sems.at[2])
    first.start()
    second.start()
    third.start()
    columns = lax.broadcasted_iota(jnp.int32, (kept, 1), 0) * block + upright(keep[...], kept)
    offsets = lax.broadcasted_iota(jnp.int32, (1, width), 1)
    for tile in range(tiles):
        piece, half = tile // halves, tile % halves
        start = ((piece * example_count + example_index) * halves + half) * width
        common = jnp.bitwise_and(start + offsets, columns)
        table[tile] = jnp.where(odd(common), -1.0, 1.0).astype(jnp.bfloat16)
    place_row = lax.broadcasted_iota(jnp.int32, (LANES, LANES), 0)
    place_col = lax.broadcasted_iota(jnp.int32, (LANES, LANES), 1)
    entry = jnp.where(odd(jnp.bitwise_and(jnp.bitwise_and(place_row, place_col), KR - 1)), -1.0, 1.0)
    low[...] = jnp.where(place_row // KR == place_col // KR, entry, 0.0).astype(jnp.bfloat16)
    first.wait()
    for piece in range(pieces):
        turned[piece] = loaded[piece].T
    second.wait()
    third.wait()


def kept_kernel(length, owners, example_count, *refs):
    params, (signs, order, starts, strides) = refs[:owners], refs[owners:]
    kept = starts.shape[0]
    each = kept // owners
    owner = lax.axis_index("context") * example_count + lax.axis_index("example")
    for key in range(owners):
        rows = pl.ds(pl.multiple_of(jnp.bitwise_xor(owner, key) * each, each), each)
        starts[rows, :] = jnp.broadcast_to(upright(params[key][0:1, :], each), (each, LANES))
        strides[rows, :] = jnp.broadcast_to(2 * upright(params[key][1:2, :], each) + 1, (each, LANES))
    lane = lax.broadcasted_iota(jnp.int32, (kept, LANES), 1)
    low = jnp.bitwise_and(lane, KR - 1)
    start, stride = starts[...], strides[...]
    inverse = stride * (2 - stride * stride)
    index = jnp.bitwise_and((low - start) * inverse, KR - 1)
    high = jnp.right_shift(jnp.bitwise_and(start + index * stride, length - 1), KR.bit_length() - 1)
    for bit in range(signs.shape[0]):
        signs[bit] = jnp.where(jnp.bitwise_and(jnp.right_shift(high, bit), 1) == 1, -1.0, 1.0)
    order[...] = jnp.bitwise_and(start + low * stride, KR - 1) + lane - low


def piece_kernel(row_key, row_count, col_keys, context_count, example_count, first, last, scale, *refs):
    rows, refs = refs[:row_count], refs[row_count:]
    cols, refs = refs[: len(col_keys)], refs[len(col_keys) :]
    turned, table, low, signs, refs = refs[0], refs[1], refs[2], refs[3], refs[4:]
    if not first:
        before, refs = refs[0], refs[1:]
    if last:
        order, refs = refs[0], refs[1:]
    outs, (gathered, projected) = refs[:-2], refs[-2:]
    sketch_index, context_index, example_index = place()
    height = gathered.shape[0]
    width = table.shape[2]
    word_rows = width // BITS
    row_piece = jnp.bitwise_xor(sketch_index, row_key)
    if row_count == 1:
        source = rows[0]
    else:
        for shift in range(row_count):
            half = jnp.bitwise_xor(example_index, shift)
            size = rows[shift].shape[0]
            gathered[pl.ds(pl.multiple_of(half * size, size), size), :] = rows[shift][...]
        source = gathered
    bit = jnp.left_shift(1, lax.broadcasted_iota(jnp.int32, (1, BITS, 1), 1))
    blocks = []
    for number, (key, shift) in enumerate(col_keys):
        piece = jnp.bitwise_xor(sketch_index, key) * context_count
        if shift is None:
            for inner in range(context_count):
                blocks.append((piece + inner, number, inner * width))
        else:
            blocks.append((piece + jnp.bitwise_xor(context_index, shift), number, 0))

    def gradient(at):
        _, number, start = blocks[at]
        return lax.dot_general(cols[number][start : start + width, :], source[...], NT, preferred_element_type=jnp.float32)

    ahead = gradient(0)
    for at in range(len(blocks)):
        now = ahead
        if at + 1 < len(blocks):
            ahead = gradient(at + 1)
        tile = blocks[at][0]
        words = turned[row_piece, pl.ds(pl.multiple_of(tile * word_rows, word_rows), word_rows), :]
        flips = jnp.bitwise_and(words[:, None, :], bit).reshape(width, height) != 0
        high, rest = split(jnp.where(flips, -now, now))
        entries = table[tile]
        part = dot(entries, high) + dot(entries, rest)
        if at == 0:
            projected[...] = part
        else:
            projected[...] += part
    groups = []
    for group in range(height // LANES):
        high, rest = split(projected[:, group * LANES : (group + 1) * LANES])
        groups.append(dot(high, low[...]) + dot(rest, low[...]))
    level = 1
    while len(groups) > 1:
        groups = [groups[at] + signs[level] * groups[at + 1] for at in range(0, len(groups), 2)]
        level += 1
    value = groups[0]
    lane = lax.broadcasted_iota(jnp.int32, value.shape, 1)
    value = jnp.where(lane >= KR, signs[0] * value, value)
    spot = row_piece * context_count + context_index
    for bit_at in range(level, signs.shape[0]):
        turn = jnp.bitwise_and(jnp.right_shift(spot, bit_at - level), 1).astype(jnp.float32)
        value = value + turn * (signs[bit_at] * value - value)
    if not first:
        value = before[...] + value
    if not last:
        outs[0][...] = value
        return
    value = jnp.take_along_axis((value + pltpu.roll(value, KR, 1)) * scale, order[...], axis=1)
    projected[:, :LANES] = value
    owner = context_index * example_count + example_index
    size = outs[0].shape[0]
    for key in range(len(outs)):
        start = pl.multiple_of(jnp.bitwise_xor(owner, key) * 2 * size, 2 * size)
        left, right = projected[pl.ds(start, size), :LANES], projected[pl.ds(start + size, size), :LANES]
        outs[key][...] = jnp.where(lane[:size] < KR, left, right)


def product_kernel(parts_count, vals_count, *refs):
    parts, vals, out, wide = refs[:parts_count], refs[parts_count : parts_count + vals_count], refs[-2], refs[-1]
    terms = [part[...] for part in parts]
    while len(terms) > 1:
        terms = [terms[at] + terms[at + 1] for at in range(0, len(terms), 2)]
    own = terms[0]
    turned = pltpu.roll(own, KR, 1)
    lane = lax.broadcasted_iota(jnp.int32, (1, LANES), 1)
    half = own.shape[0] // 2
    pairs = []
    for group in range(own.shape[0]):
        at = 2 * (group % half)
        left, right = (own, turned) if group < half else (turned, own)
        pairs.append(jnp.where(lane < KR, left[at : at + 1], right[at + 1 : at + 2]))
    wide[...] = jnp.zeros_like(wide)
    each = vals[0].shape[0]
    for number in range(vals_count):
        total = jnp.zeros((each, LANES), jnp.float32)
        for group, pair in enumerate(pairs):
            total += pair * vals[number][:, group * LANES : (group + 1) * LANES]
        first = pl.multiple_of(jnp.bitwise_xor(lax.axis_index("sketch"), number) * each, each)
        wide[pl.ds(first, each), :] = total
    wide[each * vals_count : each * vals_count + 1, :] = jnp.sum(own * own, axis=0, keepdims=True)
    out[...] = jnp.sum(wide[...].T, axis=0, keepdims=True)


def score_kernel(count, *refs):
    terms, out = [part[...] for part in refs[:-1]], refs[-1]
    while len(terms) > 1:
        terms = [terms[at] + terms[at + 1] for at in range(0, len(terms), 2)]
    out[...] = terms[0][:, :count] / jnp.sqrt(terms[0][:, count : count + 1] + 1e-06)


def call(kernel, shapes, operands, scratch=(), flops=0, moved=0, any_space=(), name=None):
    several = isinstance(shapes, (list, tuple))
    return pl.pallas_call(
        kernel,
        out_shape=shapes,
        in_specs=[HBM if at in any_space else VMEM for at in range(len(operands))],
        out_specs=[VMEM] * len(shapes) if several else VMEM,
        scratch_shapes=list(scratch),
        compiler_params=GRANT,
        cost_estimate=pl.CostEstimate(flops=flops, bytes_accessed=moved, transcendentals=0),
        name=name,
    )(*operands)


def swap(array, axes, size, key):
    return lax.ppermute(array, axes, [(at, at ^ key) for at in range(size)])


def after(arrays, *others):
    return lax.optimization_barrier((arrays, *others))[0]


def fast_body(activations, out_grads, sign_bits, keep_cols, row_start, row_step, val_sketch):
    sketch_count = lax.axis_size("sketch")
    context_count = lax.axis_size("context")
    example_count = lax.axis_size("example")
    row_piece, tokens = activations.shape[1:]
    col_piece = out_grads.shape[1]
    in_width = row_piece * sketch_count * context_count
    out_width = col_piece * sketch_count * example_count
    kept = keep_cols.shape[0]
    owners = context_count * example_count
    row_half, col_half = row_piece // example_count, col_piece // context_count
    keys = list(range(1, sketch_count))
    ahead = keys[1:] + keys[:1]
    whole = ("context", "example")
    shape = jax.ShapeDtypeStruct

    params = jnp.stack([row_start, row_step])
    keep = keep_cols.reshape(1, kept)
    out_grads, params, keep = lax.optimization_barrier((out_grads, params, keep))
    sent = share(out_grads, ahead, "context", col_half)
    got_out = {key: swap(block, "sketch", sketch_count, key) for key, block in zip(ahead, sent)}
    sent = share(activations, ahead, "example", row_half)
    got_in = {key: swap(block, "sketch", sketch_count, key) for key, block in zip(ahead, sent)}
    params = [params] + [swap(params, whole, owners, key) for key in range(1, owners)]

    words = sign_bits.reshape(sketch_count, row_piece, -1)
    tiles = sketch_count * context_count
    turned, table, low, own_in, own_out = call(
        functools.partial(table_kernel, example_count, out_width // kept),
        (
            shape((sketch_count, words.shape[2], row_piece), jnp.int32),
            shape((tiles, kept, col_half), jnp.bfloat16),
            shape((LANES, LANES), jnp.bfloat16),
            shape((row_piece, tokens), jnp.bfloat16),
            shape((col_piece, tokens), jnp.bfloat16),
        ),
        (words, keep, activations, out_grads),
        (pltpu.VMEM(words.shape, jnp.int32), pltpu.SemaphoreType.DMA((3,))),
        flops=10**9, moved=4 * 10**6, any_space=(0, 2, 3), name="tables",
    )
    high_bits = (in_width // KR).bit_length() - 1
    signs, order = call(
        functools.partial(kept_kernel, in_width, owners, example_count),
        (shape((high_bits, kept, LANES), jnp.float32), shape((kept, LANES), jnp.int32)),
        params,
        (pltpu.VMEM((kept, LANES), jnp.int32),) * 2,
        flops=10**8, moved=10**5, name="kept",
    )

    def piece_of(key, rows, cols, before, order=None):
        blocks = [own_out if shift is None else got for (_, shift), got in cols]
        width = sum(block.shape[0] for block in blocks)
        operands = [*rows, *blocks, turned, table, low, signs]
        operands += [] if before is None else [before]
        operands += [] if order is None else [order]
        out = shape((kept, LANES), jnp.float32)
        if order is not None:
            out = [shape((kept // 2 // owners, LANES), jnp.float32)] * owners
        return call(
            functools.partial(
                piece_kernel, key, len(rows), tuple(at for at, _ in cols), context_count, example_count,
                before is None, order is not None, 1.0 / math.sqrt(in_width * out_width),
            ),
            out,
            operands,
            (pltpu.VMEM((row_piece, tokens), jnp.bfloat16), pltpu.VMEM((kept, row_piece), jnp.float32)),
            flops=2 * row_piece * width * (tokens + 2 * kept), moved=2 * tokens * (row_piece + width),
            name=f"piece{key}x{len(cols)}",
        )

    own_cols = [((0, None), own_out)]
    far_cols = []
    total = piece_of(0, [own_in], own_cols, None)
    for key in ahead:
        some = [((key, 0), got_out[key])]
        some += [((key, shift), swap(got_out[key], "context", context_count, shift)) for shift in range(1, context_count)]
        far_cols += some
    total = piece_of(0, [own_in], far_cols, total)
    turns = keys[:1] + keys[1:]
    for key in turns:
        rows = [got_in[key]] + [swap(got_in[key], "example", example_count, shift) for shift in range(1, example_count)]
        total = piece_of(key, rows, own_cols + far_cols, total, order if key == turns[-1] else None)

    vals = [val_sketch]
    val_sketch = after(val_sketch, got_in[ahead[0]])
    vals += [swap(val_sketch, "sketch", sketch_count, key) for key in keys]
    parts = [total[0]] + [swap(total[key], whole, owners, key) for key in range(1, owners)]
    sums = call(
        functools.partial(product_kernel, owners, sketch_count), shape((1, LANES), jnp.float32), (*parts, *vals),
        (pltpu.VMEM((LANES, LANES), jnp.float32),), name="products",
    )
    sums = [sums] + [swap(sums, whole, owners, key) for key in range(1, owners)]
    count = val_sketch.shape[0] * sketch_count
    return call(functools.partial(score_kernel, count), shape((1, count), jnp.float32), sums, name="scores")


def fits(mesh, activations, out_grads, keep_cols, val_sketch):
    sizes = mesh.shape
    rows = activations.shape[1] // (sizes["sketch"] * sizes["context"])
    cols = out_grads.shape[1] // (sizes["sketch"] * sizes["example"])
    owners = sizes["context"] * sizes["example"]
    powers = all(size & (size - 1) == 0 for size in (*sizes.values(), rows, cols, keep_cols.shape[0]))
    whole = rows % LANES == 0 and rows // sizes["example"] >= LANES and cols // sizes["context"] >= LANES
    one = activations.shape[0] == sizes["groups"] * sizes["sketch"]
    return (
        powers and whole and one and keep_cols.shape[0] == LANES and LANES // 2 // owners >= 8
        and val_sketch.shape[0] < LANES and val_sketch.shape[0] // sizes["sketch"] >= 8
    )


def solution(mesh):
    placed = (
        P("groups", ("sketch", "context"), None),
        P("groups", ("sketch", "example"), None),
        P(None, "context", None, "example", None),
        P(),
        P(("context", "example")),
        P(("context", "example")),
        P("sketch", ("context", "example")),
    )

    def whole(*arrays):
        body = fast_body if fits(mesh, arrays[0], arrays[1], arrays[3], arrays[6]) else plain_body
        return jax.shard_map(
            body, mesh=mesh, in_specs=placed, out_specs=P(("groups", "sketch"), None), check_vma=False
        )(*arrays)

    return whole
```

```python
import functools
import math

import jax
import jax.numpy as jnp
from jax import lax
from jax.experimental import pallas as pl
from jax.experimental.pallas import tpu as pltpu
from jax.sharding import PartitionSpec as P

KR = 64
LANES = 128
BITS = 16
VMEM = pl.BlockSpec(memory_space=pltpu.VMEM)
HBM = pl.BlockSpec(memory_space=pltpu.HBM)
NT = (((1,), (1,)), ((), ()))
GRANT = pltpu.CompilerParams(vmem_limit_bytes=20 * 2**20)


def parity_sign(common, length):
    ones_total = jnp.zeros(common.shape, jnp.int32)
    for bit_place in range(max(length.bit_length() - 1, 1)):
        ones_total = ones_total + jnp.bitwise_and(jnp.right_shift(common, bit_place), 1)
    return (1 - 2 * jnp.bitwise_and(ones_total, 1)).astype(jnp.float32)


def hadamard_table(length):
    positions = jnp.arange(length, dtype=jnp.int32)
    common = jnp.bitwise_and(positions[:, None], positions[None, :])
    return parity_sign(common, length)


def hadamard_last(values):
    length = values.shape[-1]
    inner_len = min(128, length)
    outer_len = length // inner_len
    leading = values.shape[:-1]
    blocks = values.reshape(leading + (outer_len, inner_len))
    blocks = jnp.einsum(
        "...ab,bc->...ac", blocks, hadamard_table(inner_len), precision=lax.Precision.HIGHEST
    )
    blocks = jnp.einsum(
        "...ab,ac->...cb", blocks, hadamard_table(outer_len), precision=lax.Precision.HIGHEST
    )
    return blocks.reshape(values.shape) * (1.0 / math.sqrt(length))


def sign_table(packed):
    places = jnp.arange(16, dtype=jnp.int32)
    bit_values = jnp.bitwise_and(jnp.right_shift(packed[..., None], places), 1)
    return (
        (1 - 2 * bit_values)
        .astype(jnp.float32)
        .reshape(packed.shape[:-1] + (packed.shape[-1] * 16,))
    )


def plain_body(activations, out_grads, sign_bits, keep_cols, row_start, row_step, val_sketch):
    sketch_count = lax.axis_size("sketch")
    context_count = lax.axis_size("context")
    example_count = lax.axis_size("example")
    example_index = lax.axis_index("example")
    feature_piece = activations.shape[1]
    column_piece = out_grads.shape[1]
    in_width = feature_piece * sketch_count * context_count
    out_width = column_piece * sketch_count * example_count
    local_width = column_piece * sketch_count
    kept_count = keep_cols.shape[0]
    block_width = out_width // kept_count
    columns = jnp.arange(kept_count, dtype=jnp.int32) * block_width + keep_cols
    arrived_in, arrived_out = (
        lax.all_to_all(activations, "sketch", split_axis=0, concat_axis=1, tiled=True),
        lax.all_to_all(out_grads, "sketch", split_axis=0, concat_axis=1, tiled=True),
    )
    gradient = jnp.einsum(
        "edt,ekt->dk", arrived_in, arrived_out, preferred_element_type=jnp.float32
    )
    words = sign_bits.reshape(sketch_count * feature_piece, -1)
    signed = gradient * sign_table(words)
    positions = jnp.arange(local_width, dtype=jnp.int32)
    global_cols = (
        positions // column_piece * example_count + example_index
    ) * column_piece + positions % column_piece
    common = jnp.bitwise_and(global_cols[:, None], columns[None, :])
    col_table = parity_sign(common, out_width) * (1.0 / math.sqrt(out_width))
    partial_value = jnp.dot(signed, col_table, precision=lax.Precision.HIGHEST)
    rows_local = signed.shape[0]
    per_device = kept_count // (context_count * example_count)
    split_cols = partial_value.reshape(rows_local, context_count, example_count, per_device)
    moved_parts = lax.all_to_all(split_cols, "context", split_axis=1, concat_axis=0, tiled=True)
    whole_rows = lax.psum_scatter(moved_parts, "example", scatter_dimension=2, tiled=True)
    ordered = whole_rows.reshape(context_count, sketch_count, feature_piece, per_device)
    ordered = jnp.transpose(ordered, (1, 0, 2, 3)).reshape(in_width, per_device)
    column = hadamard_last(ordered.T)
    strides = 2 * row_step + 1
    kept_rows = (
        row_start[:, None] + jnp.arange(KR, dtype=jnp.int32)[None, :] * strides[:, None]
    ) % in_width
    own_sketch = jnp.take_along_axis(column, kept_rows, axis=1).reshape(1, -1)
    products = jnp.dot(
        own_sketch,
        lax.all_gather(val_sketch, "sketch", axis=0, tiled=True).T,
        precision=lax.Precision.HIGHEST,
    )
    squares = jnp.sum(own_sketch * own_sketch, axis=1)
    products, squares = lax.psum((products, squares), ("context", "example"))
    return products / jnp.sqrt(squares + 1e-06)[:, None]


def odd(values):
    for shift in (8, 4, 2, 1):
        values = jnp.bitwise_xor(values, jnp.right_shift(values, shift))
    return jnp.bitwise_and(values, 1) == 1


def split(values):
    high = values.astype(jnp.bfloat16)
    return high, (values - high.astype(jnp.float32)).astype(jnp.bfloat16)


def dot(left, right):
    return jnp.dot(left, right, preferred_element_type=jnp.float32)


def upright(row, height):
    wide = (height, row.shape[1])
    lane, sublane = lax.broadcasted_iota(jnp.int32, wide, 1), lax.broadcasted_iota(jnp.int32, wide, 0)
    chosen = jnp.where(lane == sublane, row.astype(jnp.float32), 0.0)
    return jnp.sum(chosen, axis=1, keepdims=True).astype(jnp.int32)


def targets(count, step):
    return [at ^ step for at in range(count)]


def source(step):
    return jnp.bitwise_xor(lax.axis_index("sketch"), step)


def place():
    return lax.axis_index("sketch"), lax.axis_index("context"), lax.axis_index("example")


def table_kernel(example_count, block, words, keep, turned, table, low):
    pieces = words.shape[0]
    tiles, kept, width = table.shape
    halves = tiles // pieces
    example_index = lax.axis_index("example")
    columns = lax.broadcasted_iota(jnp.int32, (kept, 1), 0) * block + upright(keep[...], kept)
    offsets = lax.broadcasted_iota(jnp.int32, (1, width), 1)
    for tile in range(tiles):
        piece, half = tile // halves, tile % halves
        start = ((piece * example_count + example_index) * halves + half) * width
        common = jnp.bitwise_and(start + offsets, columns)
        table[tile] = jnp.where(odd(common), -1.0, 1.0).astype(jnp.bfloat16)
    place_row = lax.broadcasted_iota(jnp.int32, (LANES, LANES), 0)
    place_col = lax.broadcasted_iota(jnp.int32, (LANES, LANES), 1)
    entry = jnp.where(odd(jnp.bitwise_and(jnp.bitwise_and(place_row, place_col), KR - 1)), -1.0, 1.0)
    low[...] = jnp.where(place_row // KR == place_col // KR, entry, 0.0).astype(jnp.bfloat16)
    units, _, height = turned.shape
    parts = units // pieces
    for unit in range(units):
        start = unit % parts * height
        turned[unit] = words[unit // parts, start : start + height, :].T


def kept_kernel(length, owners, example_count, *refs):
    params, (signs, order, starts, strides) = refs[:owners], refs[owners:]
    kept = starts.shape[0]
    each = kept // owners
    owner = lax.axis_index("context") * example_count + lax.axis_index("example")
    for key in range(owners):
        rows = pl.ds(pl.multiple_of(jnp.bitwise_xor(owner, key) * each, each), each)
        starts[rows, :] = jnp.broadcast_to(upright(params[key][0:1, :], each), (each, LANES))
        strides[rows, :] = jnp.broadcast_to(2 * upright(params[key][1:2, :], each) + 1, (each, LANES))
    lane = lax.broadcasted_iota(jnp.int32, (kept, LANES), 1)
    low = jnp.bitwise_and(lane, KR - 1)
    start, stride = starts[...], strides[...]
    inverse = stride * (2 - stride * stride)
    index = jnp.bitwise_and((low - start) * inverse, KR - 1)
    high = jnp.right_shift(jnp.bitwise_and(start + index * stride, length - 1), KR.bit_length() - 1)
    for bit in range(signs.shape[0]):
        signs[bit] = jnp.where(jnp.bitwise_and(jnp.right_shift(high, bit), 1) == 1, -1.0, 1.0)
    order[...] = jnp.bitwise_and(start + low * stride, KR - 1) + lane - low


def piece_kernel(row_keys, col_keys, context_count, example_count, first, last, scale, *refs):
    row_refs = len({number for number, _, _ in row_keys})
    col_refs = len({number for number, _, _ in col_keys})
    rows, refs = refs[:row_refs], refs[row_refs:]
    cols, refs = refs[:col_refs], refs[col_refs:]
    turned, table, low, signs, refs = refs[0], refs[1], refs[2], refs[3], refs[4:]
    if not first:
        before, refs = refs[0], refs[1:]
    if last:
        order, refs = refs[0], refs[1:]
    outs, projected = refs[:-1], refs[-1]
    _, context_index, example_index = place()
    height, width = turned.shape[2], table.shape[2]
    word_rows = width // BITS
    bit = jnp.left_shift(1, lax.broadcasted_iota(jnp.int32, (1, BITS, 1), 1))

    def found(entries, index, size):
        spots, seen = [], {}
        for number, key, shift in entries:
            start = seen.get(number, 0)
            seen[number] = start + 1
            part = start if shift is None else jnp.bitwise_xor(index, shift)
            spots.append((number, start * size, source(key), part))
        return spots

    row_spots = found(row_keys, example_index, height)
    col_spots = found(col_keys, context_index, width)
    pairs = [(row, col) for row in row_spots for col in col_spots]

    def gradient(pair):
        (row, row_start, _, _), (col, col_start, _, _) = pair
        left, right = cols[col][col_start : col_start + width, :], rows[row][row_start : row_start + height, :]
        return lax.dot_general(left, right, NT, preferred_element_type=jnp.float32)

    lane = lax.broadcasted_iota(jnp.int32, (LANES, LANES), 1)
    total = None
    ahead = gradient(pairs[0])
    for at, (row, col) in enumerate(pairs):
        now = ahead
        if at + 1 < len(pairs):
            ahead = gradient(pairs[at + 1])
        _, _, row_piece, row_part = row
        _, _, col_piece, col_part = col
        tile = col_piece * context_count + col_part
        word_start = pl.multiple_of(tile * word_rows, word_rows)
        words = turned[row_piece * example_count + row_part, pl.ds(word_start, word_rows), :]
        flips = jnp.bitwise_and(words[:, None, :], bit).reshape(width, height) != 0
        high, rest = split(jnp.where(flips, -now, now))
        entries = table[tile]
        part = dot(entries, high) + dot(entries, rest)
        unit = at // len(col_spots)
        if at % len(col_spots) == 0:
            projected[unit] = part
        else:
            projected[unit] += part
    for unit, (_, _, row_piece, row_part) in enumerate(row_spots):
        groups = []
        for group in range(height // LANES):
            high, rest = split(projected[unit, :, group * LANES : (group + 1) * LANES])
            groups.append(dot(high, low[...]) + dot(rest, low[...]))
        level = 1
        while len(groups) > 1:
            groups = [groups[at] + signs[level] * groups[at + 1] for at in range(0, len(groups), 2)]
            level += 1
        value = groups[0]
        spot = (row_piece * context_count + context_index) * example_count + row_part
        for bit_at in range(level, signs.shape[0]):
            turn = jnp.bitwise_and(jnp.right_shift(spot, bit_at - level), 1).astype(jnp.float32)
            value = value + turn * (signs[bit_at] * value - value)
        total = value if total is None else total + value
    value = jnp.where(lane >= KR, signs[0] * total, total)
    if not first:
        value = before[...] + value
    if not last:
        outs[0][...] = value
        return
    value = jnp.take_along_axis((value + pltpu.roll(value, KR, 1)) * scale, order[...], axis=1)
    projected[0, :, :LANES] = value
    owner = context_index * example_count + example_index
    size = outs[0].shape[0]
    for key in range(len(outs)):
        start = pl.multiple_of(jnp.bitwise_xor(owner, key) * 2 * size, 2 * size)
        left, right = projected[0, pl.ds(start, size), :LANES], projected[0, pl.ds(start + size, size), :LANES]
        outs[key][...] = jnp.where(lane[:size] < KR, left, right)


def product_kernel(parts_count, val_keys, *refs):
    parts, vals, out, wide = refs[:parts_count], refs[parts_count:-2], refs[-2], refs[-1]
    terms = [part[...] for part in parts]
    while len(terms) > 1:
        terms = [terms[at] + terms[at + 1] for at in range(0, len(terms), 2)]
    own = terms[0]
    turned = pltpu.roll(own, KR, 1)
    lane = lax.broadcasted_iota(jnp.int32, (1, LANES), 1)
    half = own.shape[0] // 2
    pairs = []
    for group in range(own.shape[0]):
        at = 2 * (group % half)
        left, right = (own, turned) if group < half else (turned, own)
        pairs.append(jnp.where(lane < KR, left[at : at + 1], right[at + 1 : at + 2]))
    wide[...] = jnp.zeros_like(wide)
    size = vals[0].shape[1]
    each, keys = size * len(vals), len(val_keys)
    blocks = []
    for shift, val in enumerate(vals):
        part = jnp.bitwise_xor(lax.axis_index("groups"), shift) * size
        blocks += [(val[at], source(key) * each + part) for at, key in enumerate(val_keys)]
    for val, first in blocks:
        size = val.shape[0]
        total = jnp.zeros((size, LANES), jnp.float32)
        for group, pair in enumerate(pairs):
            total += pair * val[:, group * LANES : (group + 1) * LANES]
        wide[pl.ds(pl.multiple_of(first, size), size), :] = total
    count = each * keys
    wide[count : count + 1, :] = jnp.sum(own * own, axis=0, keepdims=True)
    out[...] = jnp.sum(wide[...].T, axis=0, keepdims=True)


def part_kernel(whole, out):
    size = out.shape[0]
    out[...] = whole[pl.ds(pl.multiple_of(lax.axis_index("groups") * size, size), size), :]


def join_kernel(held, come, out):
    count = held.shape[0]
    out[:count] = held[...]
    out[count:] = come[...]


def score_kernel(count, *refs):
    terms, out = [part[...] for part in refs[:-1]], refs[-1]
    while len(terms) > 1:
        terms = [terms[at] + terms[at + 1] for at in range(0, len(terms), 2)]
    out[...] = terms[0][:, :count] / jnp.sqrt(terms[0][:, count : count + 1] + 1e-06)


def call(kernel, shapes, operands, scratch=(), flops=0, moved=0, any_space=()):
    several = isinstance(shapes, (list, tuple))
    return pl.pallas_call(
        kernel,
        out_shape=shapes,
        in_specs=[HBM if at in any_space else VMEM for at in range(len(operands))],
        out_specs=[VMEM] * len(shapes) if several else VMEM,
        scratch_shapes=list(scratch),
        compiler_params=GRANT,
        cost_estimate=pl.CostEstimate(flops=flops, bytes_accessed=moved, transcendentals=0),
    )(*operands)


def swap(array, axes, size, key):
    return lax.ppermute(array, axes, [(at, at ^ key) for at in range(size)])


def move(array, count, step):
    return lax.ppermute(array, "sketch", list(enumerate(targets(count, step))))


def after(arrays, *others):
    return lax.optimization_barrier((arrays, *others))[0]


def fast_body(activations, out_grads, sign_bits, keep_cols, row_start, row_step, val_sketch):
    return scored(activations, out_grads, sign_bits, keep_cols, row_start, row_step, val_sketch)


def scored(activations, out_grads, sign_bits, keep_cols, row_start, row_step, val_sketch):
    sketch_count = lax.axis_size("sketch")
    context_count = lax.axis_size("context")
    example_count = lax.axis_size("example")
    row_piece, tokens = activations.shape[1:]
    col_piece = out_grads.shape[1]
    in_width = row_piece * sketch_count * context_count
    out_width = col_piece * sketch_count * example_count
    kept = keep_cols.shape[0]
    owners = context_count * example_count
    row_half, col_half = row_piece // example_count, col_piece // context_count
    keys = list(range(1, sketch_count))
    whole = ("context", "example")
    shape = jax.ShapeDtypeStruct

    def share(array, key, axis, size):
        start = (source(key), lax.axis_index(axis) * size, 0)
        return lax.dynamic_slice(array, start, (1, size, tokens)).reshape(size, tokens)

    near, *far = keys
    sent_out = {key: share(out_grads, key, "context", col_half) for key in keys}
    got_out = {key: move(sent_out[key], sketch_count, key) for key in keys}
    sent_in = {key: share(activations, key, "example", row_half) for key in keys}
    got_in = {near: move(sent_in[near], sketch_count, near)}
    gate = got_out[far[0]]
    for key in reversed(far[1:]):
        got_in[key] = move(after(sent_in[key], gate), sketch_count, key)
        gate = got_in[key]
    group_count = lax.axis_size("groups")
    val_size = val_sketch.shape[0] // group_count
    val_shape = shape((val_size, val_sketch.shape[1]), jnp.float32)
    held = after(val_sketch, got_out[near])
    val_part = call(part_kernel, val_shape, (held,))
    joined, val_keys, step = val_part, [0], sketch_count // 2
    while step > 0:
        joined = joined.reshape(len(val_keys), *val_shape.shape)
        come = move(joined, sketch_count, step)
        val_keys += [key ^ step for key in val_keys]
        joined = call(join_kernel, shape((len(val_keys), *val_shape.shape), jnp.float32), (joined, come))
        step //= 2
    vals = [joined] + [swap(joined, "groups", group_count, shift) for shift in range(1, group_count)]
    keep = keep_cols.reshape(1, kept)

    start = (lax.axis_index("sketch"), 0, 0)
    own_in = lax.dynamic_slice(activations, start, (1, row_piece, tokens))[0]
    own_out = lax.dynamic_slice(out_grads, start, (1, col_piece, tokens))[0]
    words = sign_bits.reshape(sketch_count, row_piece, -1)
    tiles = sketch_count * context_count
    turned, table, low = call(
        functools.partial(table_kernel, example_count, out_width // kept),
        (
            shape((sketch_count * example_count, words.shape[2], row_half), jnp.int32),
            shape((tiles, kept, col_half), jnp.bfloat16),
            shape((LANES, LANES), jnp.bfloat16),
        ),
        (words, keep),
        flops=10**9, moved=4 * 10**6,
    )
    row_start, row_step = after((row_start, row_step), got_out[near])
    params = jnp.stack([row_start, row_step])
    params = [params] + [swap(params, whole, owners, key) for key in range(1, owners)]
    high_bits = (in_width // KR).bit_length() - 1
    signs, order = call(
        functools.partial(kept_kernel, in_width, owners, example_count),
        (shape((high_bits, kept, LANES), jnp.float32), shape((kept, LANES), jnp.int32)),
        params,
        (pltpu.VMEM((kept, LANES), jnp.int32),) * 2,
        flops=10**8, moved=10**5,
    )

    def piece_of(rows, cols, before, order=None):
        row_keys, col_keys = [], []
        for keyed, given, parts in ((row_keys, rows, example_count), (col_keys, cols, context_count)):
            for number, (_, key, shift) in enumerate(given):
                keyed += [(number, key, None)] * parts if shift is None else [(number, key, shift)]
        operands = [array for array, _, _ in rows + cols] + [turned, table, low, signs]
        operands += [] if before is None else [before]
        operands += [] if order is None else [order]
        out = shape((kept, LANES), jnp.float32)
        if order is not None:
            out = [shape((kept // 2 // owners, LANES), jnp.float32)] * owners
        height, width = len(row_keys) * row_half, len(col_keys) * col_half
        return call(
            functools.partial(
                piece_kernel, tuple(row_keys), tuple(col_keys), context_count, example_count,
                before is None, order is not None, 1.0 / math.sqrt(in_width * out_width),
            ),
            out,
            operands,
            (pltpu.VMEM((len(row_keys), kept, row_half), jnp.float32),),
            flops=2 * height * width * (tokens + 2 * kept), moved=2 * tokens * (height + width),
        )

    def both(array, key, axis, size, gate):
        held = after(array, gate)
        return [(array, key, 0)] + [(swap(held, axis, size, shift), key, shift) for shift in range(1, size)]

    own_rows, own_cols = [(own_in, 0, None)], [(own_out, 0, None)]
    total = piece_of(own_rows, own_cols, None)
    near_cols = both(got_out[near], near, "context", context_count, low)
    total = piece_of(own_rows, near_cols, total)
    near_rows = both(got_in[near], near, "example", example_count, total)
    total = piece_of(near_rows, own_cols + near_cols, total)
    all_cols = own_cols + near_cols
    for key in far:
        cols = both(got_out[key], key, "context", context_count, low)
        if key == far[0]:
            got_in[key] = move(after(sent_in[key], cols[-1][0]), sketch_count, key)
        total = piece_of(own_rows + near_rows, cols, total)
        all_cols = all_cols + cols
    last = far[0]
    for key in reversed(far[1:]):
        rows = both(got_in[key], key, "example", example_count, total)
        total = piece_of(rows, all_cols, total)
    mine, *others = both(got_in[last], last, "example", example_count, total)
    total = piece_of([mine], all_cols, total)
    total = piece_of(others, all_cols, total, order)

    parts = [total[0]] + [swap(total[key], whole, owners, key) for key in range(1, owners)]
    sums = call(
        functools.partial(product_kernel, owners, tuple(val_keys)), shape((1, LANES), jnp.float32), (*parts, *vals),
        (pltpu.VMEM((LANES, LANES), jnp.float32),),
    )
    sums = [sums] + [swap(sums, whole, owners, key) for key in range(1, owners)]
    count = val_sketch.shape[0] * sketch_count
    return call(functools.partial(score_kernel, count), shape((1, count), jnp.float32), sums)


def fits(mesh, activations, out_grads, keep_cols, val_sketch):
    sizes = mesh.shape
    rows = activations.shape[1] // (sizes["sketch"] * sizes["context"])
    cols = out_grads.shape[1] // (sizes["sketch"] * sizes["example"])
    owners = sizes["context"] * sizes["example"]
    powers = all(size & (size - 1) == 0 for size in (*sizes.values(), rows, cols, keep_cols.shape[0]))
    whole = rows % LANES == 0 and rows // sizes["example"] >= LANES and cols // sizes["context"] >= LANES
    one = activations.shape[0] == sizes["groups"] * sizes["sketch"]
    return (
        powers and whole and one and keep_cols.shape[0] == LANES and LANES // 2 // owners >= 8
        and val_sketch.shape[0] < LANES and val_sketch.shape[0] // (sizes["sketch"] * sizes["groups"]) >= 8
        and sizes["sketch"] >= 4
    )


def solution(mesh):
    placed = (
        P("groups", ("sketch", "context"), None),
        P("groups", ("sketch", "example"), None),
        P(None, "context", None, "example", None),
        P(),
        P(("context", "example")),
        P(("context", "example")),
        P("sketch", ("context", "example")),
    )

    def whole(*arrays):
        fast = fits(mesh, arrays[0], arrays[1], arrays[3], arrays[6])
        mapped = jax.shard_map(
            fast_body if fast else plain_body, mesh=mesh, in_specs=placed, out_specs=P(("groups", "sketch"), None),
            check_vma=False,
        )
        return mapped(*arrays)

    return whole
```
